256 devices in a mesh: dp: 4 (over y), ctx: 64 (over z, x, core).
Axes of the slice: x: 4, y: 4, z: 8, core: 2. Of those that a mesh axis runs over, the one named last changes fastest.
Arguments:
- queries: bfloat16 [4, 8192, 4096], P('dp', 'ctx'), may hold values from -80 to 80
- key_tokens: bfloat16 [4, 8192, 1024], P('dp', 'ctx'), may hold values from -80 to 80
- value_tokens: bfloat16 [4, 8192, 1024], P('dp', 'ctx'), may hold values from -6 to 6
- cotangent: bfloat16 [4, 8192, 4096], P('dp', 'ctx'), may hold values from -6 to 6
- query_map: bfloat16 [32, 128, 64], replicated, may hold values from -4 to 4
- key_map: bfloat16 [32, 128, 64], replicated, may hold values from -4 to 4
Outputs:
- attended: bfloat16 [4, 8192, 4096], P('dp', 'ctx')
- grad_query_map: float32 [32, 128, 64], replicated
- grad_key_map: float32 [32, 128, 64], replicated
The draws below stay inside these ranges and needn't reach their ends.
All inputs are finite; a program needn't handle non-finite values.
Results may differ from the reference program's by a relative error of at most 0.015.
Values sent between devices are 32-bit elements; how exact they have to be, the bound alone decides.
A program may use at most 320 MiB of HBM per device.

```python
import math
import jax
import jax.numpy as jnp
from jax import lax

HEADS = 32
KV_HEADS = 8
HEAD_DIM = 128
HALF_FEAT = 64
TOK_DEV = 128
LENGTH = 8192
SEQS = 4
N_CTX = 64


def token_rows(key, width):
    shape = (SEQS, LENGTH, width)
    return jax.random.truncated_normal(key, -6.0, 6.0, shape, jnp.float32)


def map_rows(key):
    shape = (HEADS, HEAD_DIM, HALF_FEAT)
    return jax.random.truncated_normal(key, -4.0, 4.0, shape, jnp.float32) / math.sqrt(HEAD_DIM)


def draw_queries(key, part):
    return token_rows(jax.random.fold_in(key, 11), HEADS * HEAD_DIM).astype(jnp.bfloat16)


def draw_key_tokens(key, part):
    return token_rows(jax.random.fold_in(key, 23), KV_HEADS * HEAD_DIM).astype(jnp.bfloat16)


def draw_query_map(key, part):
    return map_rows(jax.random.fold_in(key, 37)).astype(jnp.bfloat16)


def draw_key_map(key, part):
    return map_rows(jax.random.fold_in(key, 41)).astype(jnp.bfloat16)


def block_levels(own_key, dims, cuts, smallest, top_value):
    def one(dim, shards_of):
        heights = jax.random.uniform(jax.random.fold_in(jax.random.fold_in(own_key, 6), dim), (shards_of,), jnp.float32, smallest / len(cuts), top_value / len(cuts))
        return jnp.repeat(jnp.exp(heights), dims[dim] // shards_of).reshape((-1,) + (1,) * (len(dims) - dim - 1))

    loudness = one(*cuts[0])
    for cut in cuts[1:]:
        loudness = loudness * one(*cut)
    return loudness


def noise(own_key, extent, scale, limit, cuts=(), dtype=jnp.bfloat16):
    level = block_levels(own_key, extent, cuts, -0.22, 0.18) if cuts else 1.0
    array = jax.random.normal(own_key, extent, jnp.float32) * scale * level
    return jnp.minimum(jnp.maximum(array, -limit), limit).astype(dtype)


def setup_inputs(seed: int = 0) -> dict:
    key_list = jax.random.split(jax.random.key(seed), 7)
    queries = draw_queries(jax.random.fold_in(key_list[6], 71), 0)
    key_tokens = draw_key_tokens(jax.random.fold_in(key_list[6], 71), 0)
    value_tokens = noise(key_list[2], (SEQS, LENGTH, KV_HEADS * HEAD_DIM), 1.0, 6.0, ((0, 4), (1, 64)))
    cotangent = noise(key_list[3], (SEQS, LENGTH, HEADS * HEAD_DIM), 1.0, 6.0, ((0, 4), (1, 64)))
    query_map = draw_query_map(jax.random.fold_in(key_list[6], 71), 0)
    key_map = draw_key_map(jax.random.fold_in(key_list[6], 71), 0)
    return dict(queries=queries, key_tokens=key_tokens, value_tokens=value_tokens, cotangent=cotangent, query_map=query_map, key_map=key_map)


PRECISE = lax.Precision.HIGHEST


def feature_map(block_rows, weight):
    scores = jnp.einsum('lhe,hef->lhf', block_rows.astype(jnp.float32), weight.astype(jnp.float32))
    positive = jax.nn.softmax(scores, axis=-1)
    negative = jax.nn.softmax(-scores, axis=-1)
    return positive, negative, jnp.concatenate([positive, negative], axis=-1).astype(jnp.bfloat16)


def feature_back(positive, negative, upstream):
    split_at = positive.shape[-1]
    upper_half = upstream[..., :split_at]
    lower_half = upstream[..., split_at:]
    result = positive * (upper_half - jnp.sum(positive * upper_half, axis=-1, keepdims=True))
    result = result - negative * (lower_half - jnp.sum(negative * lower_half, axis=-1, keepdims=True))
    return result.astype(jnp.bfloat16)


def causal_mask(length):
    row_index = lax.broadcasted_iota(jnp.int32, (length, length), 0)
    col_index = lax.broadcasted_iota(jnp.int32, (length, length), 1)
    return row_index >= col_index


def attend(query_feat, key_feat, value_block, prefix_state, prefix_norm, causal):
    scores = jnp.einsum('thf,shf->hts', query_feat.astype(jnp.float32), key_feat.astype(jnp.float32))
    weights = jnp.where(causal[None], scores, 0.0).astype(jnp.bfloat16)
    numerator = jnp.einsum('hts,she->the', weights.astype(jnp.float32), value_block.astype(jnp.float32))
    numerator = numerator + jnp.einsum('thf,hfe->the', query_feat.astype(jnp.float32), prefix_state, precision=PRECISE)
    denominator = jnp.sum(weights.astype(jnp.float32), axis=-1).T
    denominator = denominator + jnp.einsum('thf,hf->th', query_feat.astype(jnp.float32), prefix_norm, precision=PRECISE)
    return numerator, denominator


def reference(queries, key_tokens, value_tokens, cotangent, query_map, key_map):
    causal = causal_mask(TOK_DEV)
    block_shape = (N_CTX, TOK_DEV, HEADS, HEAD_DIM)
    shared_shape = (N_CTX, TOK_DEV, KV_HEADS, HEAD_DIM)
    features = 2 * HALF_FEAT
    group_size = HEADS // KV_HEADS

    def one_sequence(inputs):
        query_seq, key_seq, value_seq, grad_seq = inputs
        query_blocks = query_seq.reshape(block_shape)
        key_blocks = jnp.repeat(key_seq.reshape(shared_shape), group_size, axis=2)
        value_blocks = jnp.repeat(value_seq.reshape(shared_shape), group_size, axis=2)
        grad_blocks = grad_seq.reshape(block_shape)

        def forward_step(carry, pieces):
            prefix_state, prefix_norm = carry
            query_block, key_block, value_block = pieces
            query_pos, query_neg, query_feat = feature_map(query_block, query_map)
            key_pos, key_neg, key_feat = feature_map(key_block, key_map)
            numerator, denominator = attend(query_feat, key_feat, value_block, prefix_state, prefix_norm, causal)
            attended = (numerator / denominator[..., None]).astype(jnp.bfloat16)
            next_state = prefix_state + jnp.einsum('shf,she->hfe', key_feat.astype(jnp.float32), value_block.astype(jnp.float32))
            next_norm = prefix_norm + jnp.sum(key_feat.astype(jnp.float32), axis=0)
            return (next_state, next_norm), (attended, prefix_state, prefix_norm)

        start = (jnp.zeros((HEADS, features, HEAD_DIM), jnp.float32), jnp.zeros((HEADS, features), jnp.float32))
        unused_carry, (attended, states, norms) = lax.scan(forward_step, start, (query_blocks, key_blocks, value_blocks))

        def backward_step(carry, pieces):
            suffix_state, suffix_norm, query_grad, key_grad = carry
            query_block, key_block, value_block, grad_block, prefix_state, prefix_norm = pieces
            query_pos, query_neg, query_feat = feature_map(query_block, query_map)
            key_pos, key_neg, key_feat = feature_map(key_block, key_map)
            numerator, denominator = attend(query_feat, key_feat, value_block, prefix_state, prefix_norm, causal)
            upstream = grad_block.astype(jnp.float32)
            scaled = (upstream / denominator[..., None]).astype(jnp.bfloat16)
            norm_grad = -jnp.sum(upstream * numerator, axis=-1) / (denominator * denominator)
            mixed = jnp.einsum('the,she->hts', scaled.astype(jnp.float32), value_block.astype(jnp.float32)) + norm_grad.T[:, :, None]
            block_grads = jnp.where(causal[None], mixed, 0.0).astype(jnp.bfloat16)
            query_feat_grad = jnp.einsum('hts,shf->thf', block_grads.astype(jnp.float32), key_feat.astype(jnp.float32))
            query_feat_grad = query_feat_grad + jnp.einsum('hfe,the->thf', prefix_state, scaled.astype(jnp.float32), precision=PRECISE)
            query_feat_grad = query_feat_grad + prefix_norm[None] * norm_grad[..., None]
            key_feat_grad = jnp.einsum('hts,thf->shf', block_grads.astype(jnp.float32), query_feat.astype(jnp.float32))
            key_feat_grad = key_feat_grad + jnp.einsum('hfe,she->shf', suffix_state, value_block.astype(jnp.float32), precision=PRECISE)
            key_feat_grad = key_feat_grad + suffix_norm[None]
            query_score_grad = feature_back(query_pos, query_neg, query_feat_grad)
            key_score_grad = feature_back(key_pos, key_neg, key_feat_grad)
            query_grad = query_grad + jnp.einsum('lhe,lhf->hef', query_block.astype(jnp.float32), query_score_grad.astype(jnp.float32))
            key_grad = key_grad + jnp.einsum('lhe,lhf->hef', key_block.astype(jnp.float32), key_score_grad.astype(jnp.float32))
            next_state = suffix_state + jnp.einsum('thf,the->hfe', query_feat.astype(jnp.float32), scaled.astype(jnp.float32))
            next_norm = suffix_norm + jnp.einsum('thf,th->hf', query_feat.astype(jnp.float32), norm_grad, precision=PRECISE)
            return (next_state, next_norm, query_grad, key_grad), None

        grad_start = (jnp.zeros((HEADS, features, HEAD_DIM), jnp.float32), jnp.zeros((HEADS, features), jnp.float32),
                      jnp.zeros((HEADS, HEAD_DIM, HALF_FEAT), jnp.float32), jnp.zeros((HEADS, HEAD_DIM, HALF_FEAT), jnp.float32))
        final, unused_out = lax.scan(backward_step, grad_start,
                                     (query_blocks, key_blocks, value_blocks, grad_blocks, states, norms), reverse=True)
        return attended.reshape(LENGTH, HEADS * HEAD_DIM), final[2], final[3]

    attended, query_grads, key_grads = lax.map(one_sequence, (queries, key_tokens, value_tokens, cotangent))
    return attended, jnp.sum(query_grads, axis=0), jnp.sum(key_grads, axis=0)
```

```python
import functools

import jax
import jax.numpy as jnp
from jax import lax
from jax.experimental import pallas as pl
from jax.experimental.pallas import tpu as pltpu
from jax.sharding import PartitionSpec as P

MESH = pl.DeviceIdType.MESH
NX, NY, NZ = 4, 4, 8
KV, GROUP, DIM, HALF = 8, 4, 128, 64
HEADS = KV * GROUP
TOK = 128
ROWS = DIM + 8
F32, BF16 = jnp.float32, jnp.bfloat16


def nn(a, b):
    return jnp.dot(a, b, preferred_element_type=F32)


def nt(a, b):
    return lax.dot_general(a, b, (((1,), (1,)), ((), ())), preferred_element_type=F32)


def split(a):
    high = a.astype(BF16)
    return high, (a - high.astype(F32)).astype(BF16)


def causal_mask():
    row = lax.broadcasted_iota(jnp.int32, (TOK, TOK), 0)
    col = lax.broadcasted_iota(jnp.int32, (TOK, TOK), 1)
    return row >= col


def softmaxes(scores):
    up = jnp.exp(scores - jnp.max(scores, axis=0, keepdims=True))
    down = jnp.exp(jnp.min(scores, axis=0, keepdims=True) - scores)
    up = up * (1.0 / jnp.sum(up, axis=0, keepdims=True))
    down = down * (1.0 / jnp.sum(down, axis=0, keepdims=True))
    return jnp.concatenate([up, down], axis=0)


def feature_back(soft, grad):
    pos, neg = soft[:HALF], soft[HALF:]
    up, low = grad[:HALF], grad[HALF:]
    result = pos * (up - jnp.sum(pos * up, axis=0, keepdims=True))
    result = result - neg * (low - jnp.sum(neg * low, axis=0, keepdims=True))
    return result.astype(BF16)


def features_kernel(q_ref, k_ref, v_ref, wq_ref, wk_ref, sq_ref, sk_ref, state_ref):
    k, v = k_ref[...], v_ref[...]
    ones = jnp.ones((8, TOK), BF16)
    for j in range(GROUP):
        soft = softmaxes(nt(wk_ref[j], k))
        sk_ref[j] = soft
        feat = soft.astype(BF16)
        state_ref[j, :DIM] = nn(feat, v)
        state_ref[j, DIM:] = nt(ones, feat)
        sq_ref[j] = softmaxes(nt(wq_ref[j], q_ref[:, j * DIM : (j + 1) * DIM]))


def attend_kernel(
    q_ref, c_ref, v_ref, sq_ref, sk_ref, prefix_ref, att_ref, suffix_ref, part_ref, gq_ref
):
    v = v_ref[...]
    causal = causal_mask()
    for j in range(GROUP):
        cols = slice(j * DIM, (j + 1) * DIM)
        soft = sq_ref[j]
        qft = soft.astype(BF16)
        qf = qft.T
        kft = sk_ref[j].astype(BF16)
        state = prefix_ref[j, :DIM]
        norm = prefix_ref[j, DIM : DIM + 1]
        high, low = split(state)
        weights = jnp.where(causal, nn(qf, kft), 0.0).astype(BF16)
        numer = nn(weights, v) + nn(qf, high) + nn(qf, low)
        qf32 = qf.astype(F32)
        denom = jnp.sum(weights.astype(F32) + qf32 * norm, axis=-1, keepdims=True)
        inv = 1.0 / denom
        attended = numer * inv
        att_ref[:, cols] = attended.astype(BF16)
        scaled32 = c_ref[:, cols].astype(F32) * inv
        scaled = scaled32.astype(BF16)
        gnorm = -jnp.sum(scaled32 * attended, axis=-1, keepdims=True)
        suffix_ref[j, :DIM] = nn(qft, scaled)
        suffix_ref[j, DIM:] = jnp.broadcast_to(
            jnp.sum(qf32 * gnorm, axis=0, keepdims=True), (8, DIM)
        )
        grads = jnp.where(causal, nt(scaled, v) + gnorm, 0.0).astype(BF16)
        part_ref[j] = nn(qft, grads)
        qgrad = nt(grads, kft) + nt(scaled, high) + nt(scaled, low) + gnorm * norm
        gq_ref[j] = nn(feature_back(soft, qgrad.T), q_ref[:, cols])


def keys_kernel(k_ref, v_ref, sk_ref, part_ref, suffix_ref, gk_ref):
    k, v = k_ref[...], v_ref[...]
    for j in range(GROUP):
        high, low = split(suffix_ref[j, :DIM])
        norm = jnp.broadcast_to(suffix_ref[j, DIM : DIM + 1], (TOK, DIM))
        kgrad = part_ref[j] + nt(high, v) + nt(low, v) + norm.T
        gk_ref[j] = nn(feature_back(sk_ref[j], kgrad), k)


def place():
    me = lax.axis_index("ctx")
    return me, me % 2, (me // 2) % NX, me // (2 * NX)


def greet(devices):
    barrier = pltpu.get_barrier_semaphore()
    for device in devices:
        pl.semaphore_signal(barrier, inc=1, device_id=device, device_id_type=MESH)
    pl.semaphore_wait(barrier, len(devices))


def send_to(source, target, send_sem, recv_sem, device):
    return pltpu.make_async_remote_copy(
        src_ref=source,
        dst_ref=target,
        send_sem=send_sem,
        recv_sem=recv_sem,
        device_id=device,
        device_id_type=MESH,
    )


def scan_kernel(
    reverse,
    st_ref,
    out_ref,
    ploc,
    chip,
    xin,
    pout,
    pin,
    zin,
    zout,
    pp,
    pf,
    s1,
    r1,
    s2,
    r2,
    s3,
    r3,
    s4,
    r4,
    s5,
    r5,
):
    me, c, x, z = place()
    dp = lax.axis_index("dp")
    partner = (dp, me + 1 - 2 * c)

    def at(z_to, x_to):
        return (dp, (z_to * NX + x_to) * 2 + c)

    xs = [(x + d) % NX for d in range(NX)]
    back = [(x + NX - d) % NX for d in range(NX)]
    z_next = (z + NZ - 1) % NZ if reverse else (z + 1) % NZ
    z_prev = (z + 1) % NZ if reverse else (z + NZ - 1) % NZ
    first = z == (NZ - 1 if reverse else 0)
    last = z == (0 if reverse else NZ - 1)
    adds_partner = c == (0 if reverse else 1)
    order = range(NX - 1, -1, -1) if reverse else range(NX)
    greet([partner] + [at(z, xs[d]) for d in range(1, NX)] + [at(z_next, x), at(z_prev, x)])

    mine, other = c * 16, (1 - c) * 16
    sends = []
    for r in range(4):
        copy = send_to(st_ref.at[pl.ds(other + r * 4, 4)], ploc.at[r], s1.at[r], r1.at[r], partner)
        copy.start()
        sends.append(copy)

    @pl.when(first)
    def _():
        zin[...] = jnp.zeros_like(zin)

    for r in range(4):
        sends[r].wait_recv()
        for j in range(4):
            chip[r, j] = st_ref[mine + r * 4 + j] + ploc[r, j]
        for d in (1, 3, 2):
            copy = send_to(
                chip.at[r, xs[d]],
                xin.at[r, x],
                s2.at[r, d - 1],
                r2.at[r, d - 1],
                at(z, xs[d]),
            )
            copy.start()
            sends.append(copy)
        xin[r, x] = chip[r, x]

    zcopies = []
    for r in range(4):
        for d in (1, 3, 2):
            send_to(
                chip.at[r, back[d]],
                xin.at[r, back[d]],
                s2.at[r, d - 1],
                r2.at[r, d - 1],
                at(z, back[d]),
            ).wait_recv()
        total = (xin[r, 0] + xin[r, 1]) + (xin[r, 2] + xin[r, 3])
        zcopy = send_to(zout.at[r], zin.at[r], s3.at[r], r3.at[r], at(z_next, x))
        zcopies.append(zcopy)

        @pl.when(jnp.logical_not(first))
        def _():
            zcopy.wait_recv()

        run = zin[r]
        zout[r] = run + total

        @pl.when(jnp.logical_not(last))
        def _():
            zcopy.start()

        for i in order:
            pout[r, i] = run
            run = run + xin[r, i]
        for d in (1, 3, 2):
            copy = send_to(
                pout.at[r, xs[d]],
                pin.at[r, x],
                s4.at[r, d - 1],
                r4.at[r, d - 1],
                at(z, xs[d]),
            )
            copy.start()
            sends.append(copy)
        pin[r, x] = pout[r, x]

    finals = []
    for r in range(4):
        for d in (1, 3, 2):
            send_to(
                pout.at[r, back[d]],
                pin.at[r, back[d]],
                s4.at[r, d - 1],
                r4.at[r, d - 1],
                at(z, back[d]),
            ).wait_recv()
        for j in range(4):
            head = mine + r * 4 + j
            base = pin[r, j]
            pp[r, j] = base + jnp.where(adds_partner, 0.0, st_ref[head])
            out_ref[head] = base + jnp.where(adds_partner, ploc[r, j], 0.0)
        copy = send_to(pp.at[r], pf.at[r], s5.at[r], r5.at[r], partner)
        copy.start()
        sends.append(copy)
        finals.append(copy)
    for r in range(4):
        finals[r].wait_recv()
        for j in range(4):
            out_ref[other + r * 4 + j] = pf[r, j]
    for copy in sends:
        copy.wait_send()

    @pl.when(jnp.logical_not(last))
    def _():
        for zcopy in zcopies:
            zcopy.wait_send()


def scan(states, reverse):
    block = (4, 4, ROWS, DIM)
    return pl.pallas_call(
        functools.partial(scan_kernel, reverse),
        out_shape=jax.ShapeDtypeStruct((HEADS, ROWS, DIM), F32),
        in_specs=[pl.BlockSpec(memory_space=pltpu.VMEM)],
        out_specs=pl.BlockSpec(memory_space=pltpu.VMEM),
        scratch_shapes=[pltpu.VMEM(block, F32)] * 5
        + [pltpu.VMEM((4, ROWS, DIM), F32)] * 2
        + [pltpu.VMEM(block, F32)] * 2
        + [pltpu.SemaphoreType.DMA((4,))] * 2
        + [pltpu.SemaphoreType.DMA((4, 3))] * 2
        + [pltpu.SemaphoreType.DMA((4,))] * 2
        + [pltpu.SemaphoreType.DMA((4, 3))] * 2
        + [pltpu.SemaphoreType.DMA((4,))] * 2,
        compiler_params=pltpu.CompilerParams(
            collective_id=1 if reverse else 0, has_side_effects=True
        ),
        name="later_scan" if reverse else "earlier_scan",
    )(states)


def reduce_kernel(
    gq_ref,
    gk_ref,
    oq_ref,
    ok_ref,
    pbuf,
    work,
    ya,
    xb,
    mid,
    xa,
    yb,
    zs,
    zr,
    zsum,
    zall,
    fa,
    fb,
    fin,
    fin2,
    sp,
    rp,
    s1,
    r1,
    s2,
    r2,
    s3,
    r3,
    s4,
    r4,
    s5,
    r5,
    s6,
    r6,
    s7,
    r7,
):
    me, c, x, z = place()
    y = lax.axis_index("dp")
    partner = (y, me + 1 - 2 * c)

    def at(y_to, z_to, x_to):
        return (y_to, (z_to * NX + x_to) * 2 + c)

    xs = [(x + d) % NX for d in range(NX)]
    xback = [(x + NX - d) % NX for d in range(NX)]
    ys = [(y + d) % NY for d in range(NY)]
    yback = [(y + NY - d) % NY for d in range(NY)]
    zs_to = [(z + d) % NZ for d in range(NZ)]
    zback = [(z + NZ - d) % NZ for d in range(NZ)]
    greet(
        [partner]
        + [at(y, z, xs[d]) for d in range(1, NX)]
        + [at(ys[d], z, x) for d in range(1, NY)]
        + [at(y, zs_to[d], x) for d in range(1, NZ)]
    )
    is_first = c == 0
    sends = []

    pair = []
    for part in range(2):
        rows = pl.ds(part * 16, 16)
        from_key = send_to(gk_ref.at[rows], pbuf.at[rows], sp.at[part], rp.at[part], partner)
        from_query = send_to(gq_ref.at[rows], pbuf.at[rows], sp.at[part], rp.at[part], partner)

        @pl.when(is_first)
        def _():
            from_key.start()

        @pl.when(jnp.logical_not(is_first))
        def _():
            from_query.start()

        pair.append(from_key)
    sends += pair

    near = (1, 3, 2)
    for part in range(2):
        pair[part].wait_recv()

        @pl.loop(0, 16)
        def _(i):
            h = part * 16 + i
            work[h] = jnp.where(is_first, gq_ref[h], gk_ref[h]) + pbuf[h]

        for d in near:
            if part == 0:
                copy = send_to(
                    work.at[pl.ds(ys[d] * 4, 4)],
                    ya.at[d - 1],
                    s1.at[0, d - 1],
                    r1.at[0, d - 1],
                    at(ys[d], z, x),
                )
            else:
                copy = send_to(
                    work.at[pl.ds(16 + xs[d] * 4, 4)],
                    xb.at[d - 1],
                    s1.at[1, d - 1],
                    r1.at[1, d - 1],
                    at(y, z, xs[d]),
                )
            copy.start()
            sends.append(copy)

    stage1 = sends[2:]
    for part in range(2):
        for copy in stage1[3 * part : 3 * part + 3]:
            copy.wait_recv()
        slots = ya if part == 0 else xb
        base = (y if part == 0 else 16 // 4 + x) * 4
        for i in range(4):
            mid[part, i] = (work[base + i] + slots[0, i]) + (slots[1, i] + slots[2, i])
        for d in near:
            if part == 0:
                copy = send_to(
                    mid.at[0, xs[d]],
                    xa.at[d - 1],
                    s2.at[0, d - 1],
                    r2.at[0, d - 1],
                    at(y, z, xs[d]),
                )
            else:
                copy = send_to(
                    mid.at[1, ys[d]],
                    yb.at[d - 1],
                    s2.at[1, d - 1],
                    r2.at[1, d - 1],
                    at(ys[d], z, x),
                )
            copy.start()
            sends.append(copy)

    stage2 = sends[8:]
    for part in range(2):
        for copy in stage2[3 * part : 3 * part + 3]:
            copy.wait_recv()
        slots = xa if part == 0 else yb
        own = x if part == 0 else y
        total = (mid[part, own] + slots[0]) + (slots[1] + slots[2])
        for i in range(NZ):
            zs[i, part] = total[i * 8 : i * 8 + 8]

    far = (1, 7, 2, 6, 3, 5, 4)
    zc = []
    for d in far:
        copy = send_to(
            zs.at[zs_to[d]], zr.at[d - 1], s3.at[d - 1], r3.at[d - 1], at(y, zs_to[d], x)
        )
        copy.start()
        zc.append(copy)
    for copy in zc:
        copy.wait_recv()
    zsum[...] = ((zs[z] + zr[0]) + (zr[1] + zr[2])) + ((zr[3] + zr[4]) + (zr[5] + zr[6]))
    sends += zc
    for d in far:
        copy = send_to(
            zsum, zall.at[z], s4.at[d - 1], r4.at[d - 1], at(y, zs_to[d], x)
        )
        copy.start()
        sends.append(copy)
    zall[z] = zsum[...]
    for d in far:
        send_to(
            zsum, zall.at[zback[d]], s4.at[d - 1], r4.at[d - 1], at(y, zback[d], x)
        ).wait_recv()

    for i in range(NZ):
        fa[x, i * 8 : i * 8 + 8] = zall[i, 0]
        fb[y, i * 8 : i * 8 + 8] = zall[i, 1]
    for part in range(2):
        for d in near:
            if part == 0:
                copy = send_to(
                    fa.at[x], fa.at[x], s5.at[0, d - 1], r5.at[0, d - 1], at(y, z, xs[d])
                )
            else:
                copy = send_to(
                    fb.at[y], fb.at[y], s5.at[1, d - 1], r5.at[1, d - 1], at(ys[d], z, x)
                )
            copy.start()
            sends.append(copy)
    for part in range(2):
        for d in near:
            if part == 0:
                send_to(
                    fa.at[xback[d]],
                    fa.at[xback[d]],
                    s5.at[0, d - 1],
                    r5.at[0, d - 1],
                    at(y, z, xback[d]),
                ).wait_recv()
            else:
                send_to(
                    fb.at[yback[d]],
                    fb.at[yback[d]],
                    s5.at[1, d - 1],
                    r5.at[1, d - 1],
                    at(yback[d], z, x),
                ).wait_recv()
        for d in near:
            if part == 0:
                copy = send_to(
                    fa, fin.at[0, y], s6.at[0, d - 1], r6.at[0, d - 1], at(ys[d], z, x)
                )
            else:
                copy = send_to(
                    fb, fin.at[1, x], s6.at[1, d - 1], r6.at[1, d - 1], at(y, z, xs[d])
                )
            copy.start()
            sends.append(copy)
    fin[0, y] = fa[...]
    fin[1, x] = fb[...]
    last = []
    for part in range(2):
        for d in near:
            if part == 0:
                send_to(
                    fa, fin.at[0, yback[d]], s6.at[0, d - 1], r6.at[0, d - 1], at(yback[d], z, x)
                ).wait_recv()
            else:
                send_to(
                    fb, fin.at[1, xback[d]], s6.at[1, d - 1], r6.at[1, d - 1], at(y, z, xback[d])
                ).wait_recv()
        copy = send_to(fin.at[part], fin2.at[part], s7.at[part], r7.at[part], partner)
        copy.start()
        last.append(copy)
    for part in range(2):
        last[part].wait_recv()
        for i in range(4):
            @pl.loop(0, 4)
            def _(j):
                h = part * 16 + i * 4 + j
                own, got = fin[part, i, j], fin2[part, i, j]
                oq_ref[h] = jnp.where(is_first, own, got).T
                ok_ref[h] = jnp.where(is_first, got, own).T

    for copy in sends + last:
        copy.wait_send()


def reduce_all(gq, gk):
    piece = (HALF, DIM)
    dma = pltpu.SemaphoreType.DMA
    return pl.pallas_call(
        reduce_kernel,
        out_shape=[jax.ShapeDtypeStruct((HEADS, DIM, HALF), F32)] * 2,
        in_specs=[pl.BlockSpec(memory_space=pltpu.VMEM)] * 2,
        out_specs=[pl.BlockSpec(memory_space=pltpu.VMEM)] * 2,
        scratch_shapes=[
            pltpu.VMEM((HEADS,) + piece, F32),
            pltpu.VMEM((HEADS,) + piece, F32),
            pltpu.VMEM((3, 4) + piece, F32),
            pltpu.VMEM((3, 4) + piece, F32),
            pltpu.VMEM((2, 4) + piece, F32),
            pltpu.VMEM((3,) + piece, F32),
            pltpu.VMEM((3,) + piece, F32),
            pltpu.VMEM((NZ, 2, 8, DIM), F32),
            pltpu.VMEM((NZ - 1, 2, 8, DIM), F32),
            pltpu.VMEM((2, 8, DIM), F32),
            pltpu.VMEM((NZ, 2, 8, DIM), F32),
            pltpu.VMEM((4,) + piece, F32),
            pltpu.VMEM((4,) + piece, F32),
            pltpu.VMEM((2, 4, 4) + piece, F32),
            pltpu.VMEM((2, 4, 4) + piece, F32),
        ]
        + [dma((2,))] * 2
        + [dma((2, 3))] * 4
        + [dma((NZ - 1,))] * 4
        + [dma((2, 3))] * 4
        + [dma((2,))] * 2,
        compiler_params=pltpu.CompilerParams(collective_id=2, has_side_effects=True),
        name="reduce_maps",
    )(gq, gk)


def wide():
    return pl.BlockSpec((TOK, GROUP * DIM), lambda g: (0, g))


def narrow():
    return pl.BlockSpec((TOK, DIM), lambda g: (0, g))


def per_head(rows):
    return pl.BlockSpec((GROUP, rows, DIM), lambda g: (g, 0, 0))


def heads_of(rows):
    return jax.ShapeDtypeStruct((HEADS, rows, DIM), F32)


def shards(queries, key_tokens, value_tokens, cotangent, query_map, key_map):
    q, k, v, c = queries[0], key_tokens[0], value_tokens[0], cotangent[0]
    wq = jnp.swapaxes(query_map, 1, 2)
    wk = jnp.swapaxes(key_map, 1, 2)
    soft_q, soft_k, state = pl.pallas_call(
        features_kernel,
        grid=(KV,),
        in_specs=[wide(), narrow(), narrow(), per_head(HALF), per_head(HALF)],
        out_specs=[per_head(DIM), per_head(DIM), per_head(ROWS)],
        out_shape=[heads_of(DIM), heads_of(DIM), heads_of(ROWS)],
        name="features",
    )(q, k, v, wq, wk)
    prefix = scan(state, False)
    attended, suffix_part, key_part, gq = pl.pallas_call(
        attend_kernel,
        grid=(KV,),
        in_specs=[
            wide(),
            wide(),
            narrow(),
            per_head(DIM),
            per_head(DIM),
            per_head(ROWS),
        ],
        out_specs=[wide(), per_head(ROWS), per_head(DIM), per_head(HALF)],
        out_shape=[
            jax.ShapeDtypeStruct(q.shape, BF16),
            heads_of(ROWS),
            heads_of(DIM),
            heads_of(HALF),
        ],
        name="attend",
    )(q, c, v, soft_q, soft_k, prefix)
    suffix = scan(suffix_part, True)
    gk = pl.pallas_call(
        keys_kernel,
        grid=(KV,),
        in_specs=[narrow(), narrow(), per_head(DIM), per_head(DIM), per_head(ROWS)],
        out_specs=per_head(HALF),
        out_shape=heads_of(HALF),
        name="keys",
    )(k, v, soft_k, key_part, suffix)
    query_grad, key_grad = reduce_all(gq, gk)
    return attended[None], query_grad, key_grad


def solution(mesh):
    in_specs = (
        P("dp", "ctx", None),
        P("dp", "ctx", None),
        P("dp", "ctx", None),
        P("dp", "ctx", None),
        P(),
        P(),
    )
    out_specs = (P("dp", "ctx", None), P(), P())
    return jax.shard_map(shards, mesh=mesh, in_specs=in_specs, out_specs=out_specs, check_vma=False)
```
